256 devices in a mesh: ctx: 32 (over y, z), head: 8 (over x, core).
Axes of the slice: x: 4, y: 4, z: 8, core: 2. Of those that a mesh axis runs over, the one named last changes fastest.
Arguments:
- queries: bfloat16 [16384, 8192], P('ctx', 'head'), may hold values from -6 to 6
- keys: bfloat16 [16384, 8192], P('ctx', 'head'), may hold values from -6 to 6
- values: bfloat16 [16384, 8192], P('ctx', 'head'), may hold values from -36 to 36
- out_grad: bfloat16 [16384, 8192], P('ctx', 'head'), may hold values from -6 to 6
- gain: float32 [8192], P('head'), may hold values from 0.25 to 1.75
- decay_rate: int32 [64], P('head'), may hold values from 9 to 42
- doc_lengths: int32 [8], replicated, may hold values from 1 to 10240, 16384 in all
Outputs:
- normed: bfloat16 [16384, 8192], P('ctx', 'head')
- query_grad: bfloat16 [16384, 8192], P('ctx', 'head')
- key_grad: bfloat16 [16384, 8192], P('ctx', 'head')
- value_grad: bfloat16 [16384, 8192], P('ctx', 'head')
The draws below stay inside these ranges and needn't reach their ends.
Inputs may be any that keep to these rules, and one draw needn't show every extreme that they name: `doc_lengths`: the documents fill the 16384 positions in order; the longest has exactly 10240 positions.
All inputs are finite; a program needn't handle non-finite values.
Results may differ from the reference program's by a relative error of at most 0.0056.
Values sent between devices are 32-bit elements; how exact they have to be, the bound alone decides.
A program may use at most 128 MiB of HBM per device.

```python
import math
import jax
import jax.numpy as jnp
import numpy as np
from jax import lax

HEADS = 64
HD = 128
TOK_DEV = 512
DOCS = 8
TOKENS = 16384
LONGEST = 10240
N_CTX = 32


def draw_values(key, part):
    columns = jnp.arange(HEADS * HD) // HD
    fraction = columns.astype(jnp.float32) / max(HEADS - 1, 1)
    base = jnp.clip(jax.random.normal(key, (TOKENS, HEADS * HD), jnp.float32), -4.0, 4.0)
    scale = 3.0 ** fraction
    return (base * scale[None, :]).astype(jnp.bfloat16)


def with_ends(result, stream_key, low, high):
    extent = result.shape
    place = [jax.random.randint(jax.random.fold_in(stream_key, axis), (), 0, extent[axis]) for axis in range(len(extent))]
    result = result.at[tuple(place)].set(low)
    longest = extent.index(max(extent))
    place[longest] = (place[longest] + 1) % extent[longest]
    return result.at[tuple(place)].set(high)


def levels(key, shape, shards, least, largest):
    loudness, own = 1.0, jax.random.fold_in(key, 6)
    for dim, shards_of in shards:
        heights = jnp.exp(jax.random.uniform(jax.random.fold_in(own, dim), (shards_of,), jnp.float32, least / len(shards), largest / len(shards)))
        loudness = loudness * jnp.repeat(heights, shape[dim] // shards_of).reshape([-1 if axis == dim else 1 for axis in range(len(shape))])
    return loudness


def split_up(number_of, total, most, skew):
    portions = [(1 << 20) // math.isqrt(grade ** skew) + 1 for grade in range(2, number_of + 1)]
    rest, holding = total - most - (number_of - 1), [1] * (number_of - 1)
    while rest > 0:
        movable = [i for i in range(number_of - 1) if holding[i] < most]
        mass, budget = sum([portions[i] for i in movable]), rest
        for i in movable:
            more = min(most - holding[i], max(1, budget * portions[i] // mass), rest)
            holding[i] = holding[i] + more
            rest = rest - more
    return np.array([most] + holding)


def ragged(key, count, total, most, slope):
    if count == 2:
        one = jax.random.randint(key, (), max(1, total - most), min(most, total - 1) + 1)
        return jnp.stack([one, total - one])
    tallies = jnp.asarray(split_up(count, total, most, slope), jnp.int32)
    twos = (count - 1) // 2
    giver, taker = tallies[1:1 + 2 * twos:2], tallies[2:2 + 2 * twos:2]
    margin = jnp.minimum(giver - 1, most - taker)
    moved = jax.random.randint(jax.random.fold_in(key, 1), (twos,), 0, 1 << 20) % (margin + 1)
    tallies = tallies.at[1:1 + 2 * twos:2].set(giver - moved).at[2:2 + 2 * twos:2].set(taker + moved)
    return tallies[jax.random.permutation(jax.random.fold_in(key, 2), count)]


def gaussian(rng, extent, scale, most, shards=(), held_as=jnp.bfloat16):
    entries = scale * jax.random.normal(rng, extent, jnp.float32)
    if shards:
        entries = entries * levels(rng, extent, shards, -0.22, 0.18)
    return jnp.clip(entries, -most, most).astype(held_as)


def setup_inputs(seed: int = 0) -> dict:
    arg_keys = jax.random.split(jax.random.key(seed), 8)
    queries = gaussian(arg_keys[0], (TOKENS, HEADS * HD), 1.0, 6.0, ((0, 32), (1, 8)))
    keys = gaussian(arg_keys[1], (TOKENS, HEADS * HD), 1.0, 6.0, ((0, 32), (1, 8)))
    values = draw_values(jax.random.fold_in(arg_keys[7], 71), 0)
    out_grad = gaussian(arg_keys[3], (TOKENS, HEADS * HD), 1.0, 6.0, ((0, 32), (1, 8)))
    gain = jnp.clip(1.0 + 0.15 * jax.random.normal(arg_keys[4], (HEADS * HD,), jnp.float32), 0.25, 1.75)
    decay_rate = with_ends(jax.random.randint(arg_keys[5], (HEADS,), 9, 43), jax.random.fold_in(arg_keys[5], 1), 9, 42).astype(jnp.int32)
    doc_lengths = ragged(arg_keys[6], DOCS, TOKENS, LONGEST, 2).astype(jnp.int32)
    return {"queries": queries, "keys": keys, "values": values, "out_grad": out_grad, "gain": gain, "decay_rate": decay_rate, "doc_lengths": doc_lengths}


FULL_PRECISION = lax.Precision.HIGHEST
EPSILON = 1e-05

def document_ids(positions, lengths):
    ends = jnp.cumsum(lengths).astype(jnp.int32)
    return lax.optimization_barrier(jnp.sum((positions[:, None] >= ends[None, :]).astype(jnp.int32), axis=1))

def block_flags(starts, block_rows, lengths):
    last_doc = document_ids(starts + block_rows - 1, lengths)
    before_doc = document_ids(jnp.maximum(starts - 1, 0), lengths)
    before_doc = jnp.where(starts > 0, before_doc, -1)
    return (last_doc, before_doc)

def decay_tables(start, block_rows, lengths, log_decay):
    positions = start + jnp.arange(block_rows, dtype=jnp.int32)
    row_docs = document_ids(positions, lengths)
    last_doc, before_doc = block_flags(start[None], block_rows, lengths)
    alive = row_docs == before_doc[0]
    reach = row_docs == last_doc[0]
    offsets = jnp.arange(block_rows).astype(jnp.float32)
    spacing = offsets[:, None] - offsets[None, :]
    causal = (spacing >= 0) & (row_docs[:, None] == row_docs[None, :])
    inner_decay = jnp.where(causal[None], jnp.exp(jnp.maximum(spacing, 0.0)[None] * log_decay[:, None, None]), 0.0)
    entry_decay = jnp.where(alive[None], jnp.exp((offsets + 1.0)[None] * log_decay[:, None]), 0.0)
    exit_decay = jnp.where(reach[None], jnp.exp((block_rows - 1.0 - offsets)[None] * log_decay[:, None]), 0.0)
    carry_decay = jnp.exp(block_rows * log_decay) * alive[block_rows - 1].astype(jnp.float32)
    return (inner_decay, entry_decay, exit_decay, carry_decay)

def mix(form, left, right):
    return jnp.einsum(form, left.astype(jnp.float32), right.astype(jnp.float32), precision=FULL_PRECISION)

def reference(queries, keys, values, out_grad, gain, decay_rate, doc_lengths):
    log_decay = -jnp.exp2(-decay_rate.astype(jnp.float32) / 2.0)
    layout = (N_CTX, TOK_DEV, HEADS, HD)
    gain_heads = gain.reshape(HEADS, HD)
    features = HEADS * HD

    def forward(state_before, block):
        index, query_rows, key_rows, value_rows, grad_rows = block
        start = (index * TOK_DEV).astype(jnp.int32)
        inner_decay, entry_decay, exit_decay, carry_decay = decay_tables(start, TOK_DEV, doc_lengths, log_decay)
        entry_t = entry_decay.T[:, :, None]
        exit_t = exit_decay.T[:, :, None]
        weights = (mix('thd,shd->hts', query_rows, key_rows) * inner_decay).astype(jnp.bfloat16)
        key_scaled = (key_rows.astype(jnp.float32) * exit_t).astype(jnp.bfloat16)
        local_state = mix('thd,the->hde', key_scaled, value_rows)
        attended = mix('hts,she->the', weights, value_rows) + entry_t * mix('thd,hde->the', query_rows, state_before)
        square_sum = lax.optimization_barrier(jnp.sum(attended * attended, axis=(1, 2)))
        grad_gain = grad_rows.astype(jnp.float32) * gain_heads[None]
        dot_sum = lax.optimization_barrier(jnp.sum(grad_gain * attended, axis=(1, 2)))
        inv_rms = lax.rsqrt(square_sum / features + EPSILON)[:, None, None]
        normed = (attended * inv_rms * gain_heads[None]).astype(jnp.bfloat16)
        grad_out = (inv_rms * (grad_gain - attended * (inv_rms * inv_rms) * dot_sum[:, None, None] / features)).astype(jnp.bfloat16)
        grad_weights = (mix('the,she->hts', grad_out, value_rows) * inner_decay).astype(jnp.bfloat16)
        query_scaled = (query_rows.astype(jnp.float32) * entry_t).astype(jnp.bfloat16)
        local_grad = mix('thd,the->hde', query_scaled, grad_out)
        query_grad = (mix('hts,shd->thd', grad_weights, key_rows) + entry_t * mix('the,hde->thd', grad_out, state_before)).astype(jnp.bfloat16)
        key_part = mix('hts,thd->shd', grad_weights, query_rows)
        value_part = mix('hts,the->she', weights, grad_out)
        state_after = carry_decay[:, None, None] * state_before + local_state
        return (state_after, (normed, query_grad, key_part, value_part, local_grad, exit_decay, carry_decay))
    query_all = queries.reshape(layout)
    key_all = keys.reshape(layout)
    value_all = values.reshape(layout)
    grad_all = out_grad.reshape(layout)
    start_state = jnp.zeros((HEADS, HD, HD), jnp.float32)
    indices = jnp.arange(N_CTX, dtype=jnp.int32)
    _, saved = lax.scan(forward, start_state, (indices, query_all, key_all, value_all, grad_all))
    normed, query_grad, key_part, value_part, local_grad, exit_decay, carry_decay = saved

    def backward(grad_after, block):
        key_rows, value_rows, key_piece, value_piece, grad_local, exit_here, carry_here = block
        exit_t = exit_here.T[:, :, None]
        key_grad = (key_piece + exit_t * mix('she,hde->shd', value_rows, grad_after)).astype(jnp.bfloat16)
        value_grad = (value_piece + exit_t * mix('shd,hde->she', key_rows, grad_after)).astype(jnp.bfloat16)
        return (grad_local + carry_here[:, None, None] * grad_after, (key_grad, value_grad))
    _, (key_grad, value_grad) = lax.scan(backward, start_state, (key_all, value_all, key_part, value_part, local_grad, exit_decay, carry_decay), reverse=True)
    flat = (TOKENS, HEADS * HD)
    return (normed.reshape(flat), query_grad.reshape(flat), key_grad.reshape(flat), value_grad.reshape(flat))
```

```python
import jax
import jax.numpy as jnp
from jax import lax
from jax.experimental import pallas as pl
from jax.experimental.pallas import tpu as pltpu
from jax.sharding import PartitionSpec as P

EPSILON = 1e-05
FAR = 1e30
TILE = 256
MESH = pl.DeviceIdType.MESH
F32, BF16 = jnp.float32, jnp.bfloat16


def matmul(a, b):
    return lax.dot_general(a, b, (((1,), (0,)), ((), ())), preferred_element_type=F32)


def matmul_t(a, b):
    return lax.dot_general(a, b, (((1,), (1,)), ((), ())), preferred_element_type=F32)


def halves(x):
    high = x.astype(BF16)
    low = (x - high.astype(F32)).astype(BF16)
    return high, low


def twice(x):
    return jnp.concatenate([x, x], axis=1)


def make_kernel(n_ctx, n_head, n_y, n_z, rows, heads, hd, features):
    rows_own = heads * hd // n_ctx
    owners = hd // rows_own
    away = [(dy, dz) for dy in range(n_y) for dz in range(n_z) if (dy, dz) != (0, 0)]
    away.sort(key=lambda d: -(min(d[0], n_y - d[0]) + 1.01 * min(d[1], n_z - d[1])))

    def kernel(
        lengths, rates, gain, q_hbm, k_hbm, v_hbm, g_hbm,
        normed_hbm, qg_hbm, kg_hbm, vg_hbm,
        q, k, v, g, normed, qg, kg, vg,
        local1, inbox1, outbox1, state1, local2, inbox2, outbox2, state2,
        weights, attended, grad_out, spacing, entry_far, exit_far,
        square_acc, dot_acc, part, parts, key_part, value_part, carry_table,
        in_sem, out_sem, send1, recv1, send2, recv2, send3, recv3, send4, recv4, send_p, recv_p,
    ):
        me = lax.axis_index("ctx")
        me_h = lax.axis_index("head")
        y, z = me // n_z, me % n_z
        peers = [((y + dy) % n_y) * n_z + (z + dz) % n_z for dy, dz in away]

        loads = [
            pltpu.make_async_copy(src, dst, in_sem.at[i])
            for i, (src, dst) in enumerate(((k_hbm, k), (v_hbm, v), (q_hbm, q), (g_hbm, g)))
        ]
        for load in loads:
            load.start()
        barrier = pltpu.get_barrier_semaphore()
        for peer in peers:
            pl.semaphore_signal(barrier, inc=1, device_id={"ctx": peer}, device_id_type=MESH)
        for step in range(1, n_head):
            pl.semaphore_signal(
                barrier, inc=1, device_id={"head": (me_h + step) % n_head}, device_id_type=MESH
            )

        ends = []
        total = jnp.int32(0)
        for j in range(lengths.shape[0]):
            total = total + lengths[j]
            ends.append(total)

        def doc_of(position):
            count = (position >= ends[0]).astype(jnp.int32)
            for end in ends[1:]:
                count = count + (position >= end).astype(jnp.int32)
            return count

        start = me * rows
        last_doc = doc_of(start + rows - 1)
        before_doc = jnp.where(start > 0, doc_of(start - 1), -1)
        offset = lax.broadcasted_iota(jnp.int32, (rows, hd), 0)
        doc_col = doc_of(start + offset)
        offset_f = offset.astype(F32)
        entry_far[...] = jnp.where(doc_col == before_doc, offset_f + 1.0, FAR)
        exit_far[...] = jnp.where(doc_col == last_doc, rows - 1.0 - offset_f, FAR)

        def decay_row(h):
            rate = rates[h].astype(F32)
            return -jnp.exp2(jnp.full((1, hd), 1.0, F32) * (rate * -0.5))

        def cols(h):
            return pl.ds(pl.multiple_of(h * hd, hd), hd)

        own_head = me // owners
        block = lax.broadcasted_iota(jnp.int32, (n_ctx, hd), 0)
        inside = jnp.zeros((n_ctx, hd), jnp.int32)
        for end in ends:
            hit = (end >= block * rows) & (end < block * rows + rows)
            inside = inside + hit.astype(jnp.int32)
        whole = (inside == 0) & (block > 0)
        carry_table[...] = jnp.where(whole, jnp.exp(decay_row(own_head) * float(rows)), 0.0)

        loads[0].wait()
        loads[1].wait()

        @pl.loop(0, heads)
        def _(h):
            fade = jnp.exp(exit_far[...] * decay_row(h))
            scaled = (k[:, cols(h)].astype(F32) * fade).astype(BF16)
            state = matmul(scaled.T, v[:, cols(h)])
            local1[pl.ds(h * owners, owners)] = state.reshape(owners, rows_own, hd)

        pl.semaphore_wait(barrier, n_ctx - 1 + n_head - 1)

        def spread(src, dst, send, recv):
            for peer in peers:
                pltpu.make_async_remote_copy(
                    src_ref=src.at[peer], dst_ref=dst.at[me], send_sem=send.at[peer],
                    recv_sem=recv.at[me], device_id={"ctx": peer}, device_id_type=MESH,
                ).start()

        def arrived(dst, recv, send, slot):
            pltpu.make_async_remote_copy(
                src_ref=dst.at[slot], dst_ref=dst.at[slot], send_sem=send.at[slot],
                recv_sem=recv.at[slot], device_id={"ctx": slot}, device_id_type=MESH,
            ).wait_recv()

        def arrived_all(dst, recv, send):
            for peer in peers:
                arrived(dst, recv, send, peer)

        def left_all(src, dst, send, recv):
            for peer in peers:
                pltpu.make_async_remote_copy(
                    src_ref=src.at[peer], dst_ref=dst.at[me], send_sem=send.at[peer],
                    recv_sem=recv.at[me], device_id={"ctx": peer}, device_id_type=MESH,
                ).wait_send()

        spread(local1, inbox1, send1, recv1)
        inbox1[pl.ds(me, 1)] = local1[pl.ds(me, 1)]

        row_pos = start + lax.broadcasted_iota(jnp.int32, (8, rows), 1)
        doc_row = doc_of(row_pos)[0:1]
        for c in range(rows // hd):
            piece = slice(c * hd, (c + 1) * hd)
            gap = offset - (lax.broadcasted_iota(jnp.int32, (rows, hd), 1) + c * hd)
            same = (doc_col == doc_row[:, piece]) & (gap >= 0)
            spacing[:, piece] = jnp.where(same, gap.astype(F32), FAR)
        loads[2].wait()
        loads[3].wait()

        tiles = [(i * TILE, (i + 1) * TILE) for i in range(rows // TILE)]

        def wide(row, n):
            return jnp.concatenate([row] * (n // hd), axis=1)

        def forward(h):
            rate = decay_row(h)
            key_h, value_h = k[:, cols(h)], v[:, cols(h)]
            for lo, hi in tiles:
                scores = matmul_t(q[lo:hi, cols(h)], key_h[:hi])
                inner = jnp.exp(spacing[lo:hi, :hi] * wide(rate, hi))
                w = (scores * inner).astype(BF16)
                weights[h, lo:hi, :hi] = w
                attended[lo:hi, cols(h)] = matmul(w, value_h[:hi])

        half = heads // 2

        @pl.loop(0, half)
        def _(h):
            forward(h)

        arrived_all(inbox1, recv1, send1)

        def prefix(inbox, outbox, state, reverse):
            def lap(i, carried):
                j = n_ctx - 1 - i if reverse else i
                outbox[pl.ds(j, 1)] = carried[None]
                return carried * carry_table[pl.ds(j, 1), :] + inbox[j]

            lax.fori_loop(0, n_ctx, lap, jnp.zeros((rows_own, hd), F32))
            state[pl.ds(me, 1)] = outbox[pl.ds(me, 1)]

        prefix(inbox1, outbox1, state1, False)
        spread(outbox1, state1, send2, recv2)

        @pl.loop(half, heads)
        def _(h):
            forward(h)

        arrived_all(state1, recv2, send2)
        square_acc[...] = jnp.zeros_like(square_acc)
        dot_acc[...] = jnp.zeros_like(dot_acc)

        @pl.loop(0, heads)
        def _(h):
            high, low = halves(state1[pl.ds(h * owners, owners)].reshape(hd, hd))
            far = matmul(twice(q[:, cols(h)]), jnp.concatenate([high, low], axis=0))
            fade = jnp.exp(entry_far[...] * decay_row(h))
            att = attended[:, cols(h)] + fade * far
            attended[:, cols(h)] = att
            square_acc[...] += att * att
            dot_acc[...] += (g[:, cols(h)].astype(F32) * gain[pl.ds(h, 1), :]) * att

        def row_sums(x):
            return jnp.broadcast_to(jnp.sum(x, axis=1, keepdims=True), x.shape).T[0:8]

        first = lax.broadcasted_iota(jnp.int32, (8, rows), 0) < 4
        part[...] = jnp.where(first, row_sums(square_acc[...]), row_sums(dot_acc[...]))

        def part_copy(step):
            peer = (me_h + step) % n_head
            return pltpu.make_async_remote_copy(
                src_ref=part, dst_ref=parts.at[me_h], send_sem=send_p.at[peer],
                recv_sem=recv_p.at[me_h], device_id={"head": peer}, device_id_type=MESH,
            )

        for step in range(1, n_head):
            part_copy(step).start()
        parts[pl.ds(me_h, 1)] = part[...][None]
        for step in range(1, n_head):
            peer = (me_h + step) % n_head
            pltpu.make_async_remote_copy(
                src_ref=part, dst_ref=parts.at[peer], send_sem=send_p.at[peer],
                recv_sem=recv_p.at[peer], device_id={"head": peer}, device_id_type=MESH,
            ).wait_recv()
        total_part = parts[0]
        for slot in range(1, n_head):
            total_part = total_part + parts[slot]
        inv_row = lax.rsqrt(total_part[0:4] / features + EPSILON)
        pull_row = (inv_row * inv_row) * total_part[4:8] / features
        both = jnp.concatenate([inv_row, pull_row], axis=0)
        turned = jnp.concatenate([both] * (hd // 8), axis=0).T
        inv = jnp.broadcast_to(turned[:, 0:1], (rows, hd))
        pull = jnp.broadcast_to(turned[:, 4:5], (rows, hd))
        square_acc[...] = inv
        dot_acc[...] = pull

        @pl.loop(0, heads)
        def _(h):
            inv, pull = square_acc[...], dot_acc[...]
            att = attended[:, cols(h)]
            gain_h = gain[pl.ds(h, 1), :]
            grad_gain = g[:, cols(h)].astype(F32) * gain_h
            normed[:, cols(h)] = (att * inv * gain_h).astype(BF16)
            grad_h = (inv * (grad_gain - att * pull)).astype(BF16)
            grad_out[:, cols(h)] = grad_h
            fade = jnp.exp(entry_far[...] * decay_row(h))
            scaled = (q[:, cols(h)].astype(F32) * fade).astype(BF16)
            local2[pl.ds(h * owners, owners)] = matmul(scaled.T, grad_h).reshape(
                owners, rows_own, hd
            )

        spread(local2, inbox2, send3, recv3)
        inbox2[pl.ds(me, 1)] = local2[pl.ds(me, 1)]
        outs = [
            pltpu.make_async_copy(src, dst, out_sem.at[i])
            for i, (src, dst) in enumerate(
                ((normed, normed_hbm), (qg, qg_hbm), (kg, kg_hbm), (vg, vg_hbm))
            )
        ]
        outs[0].start()

        def backward(h):
            rate = decay_row(h)
            grad_h, key_h, value_h = grad_out[:, cols(h)], k[:, cols(h)], v[:, cols(h)]
            query_t, grad_t = q[:, cols(h)].T, grad_h.T
            high, low = halves(state1[pl.ds(h * owners, owners)].reshape(hd, hd))
            far = matmul_t(twice(grad_h), jnp.concatenate([high, low], axis=1))
            fade = jnp.exp(entry_far[...] * rate)
            far = far * fade
            key_sum = jnp.zeros((hd, rows), F32)
            value_sum = jnp.zeros((hd, rows), F32)
            for lo, hi in tiles:
                scores = matmul_t(grad_h[lo:hi], value_h[:hi])
                inner = jnp.exp(spacing[lo:hi, :hi] * wide(rate, hi))
                gw = (scores * inner).astype(BF16)
                qg[lo:hi, cols(h)] = (matmul(gw, key_h[:hi]) + far[lo:hi]).astype(BF16)
                key_add = matmul(query_t[:, lo:hi], gw)
                value_add = matmul(grad_t[:, lo:hi], weights[h, lo:hi, :hi])
                if hi < rows:
                    rest = jnp.zeros((hd, rows - hi), F32)
                    key_add = jnp.concatenate([key_add, rest], axis=1)
                    value_add = jnp.concatenate([value_add, rest], axis=1)
                key_sum = key_sum + key_add
                value_sum = value_sum + value_add
            key_part[:, cols(h)] = key_sum.T
            value_part[:, cols(h)] = value_sum.T

        @pl.loop(0, half)
        def _(h):
            backward(h)

        arrived_all(inbox2, recv3, send3)
        prefix(inbox2, outbox2, state2, True)
        spread(outbox2, state2, send4, recv4)

        @pl.loop(half, heads)
        def _(h):
            backward(h)

        outs[1].start()
        arrived_all(state2, recv4, send4)

        @pl.loop(0, heads)
        def _(h):
            high, low = halves(state2[pl.ds(h * owners, owners)].reshape(hd, hd))
            fade = jnp.exp(exit_far[...] * decay_row(h))
            key_far = matmul_t(twice(v[:, cols(h)]), jnp.concatenate([high, low], axis=1))
            value_far = matmul(twice(k[:, cols(h)]), jnp.concatenate([high, low], axis=0))
            kg[:, cols(h)] = (key_part[:, cols(h)] + fade * key_far).astype(BF16)
            vg[:, cols(h)] = (value_part[:, cols(h)] + fade * value_far).astype(BF16)

        outs[2].start()
        outs[3].start()
        left_all(local1, inbox1, send1, recv1)
        left_all(outbox1, state1, send2, recv2)
        left_all(local2, inbox2, send3, recv3)
        left_all(outbox2, state2, send4, recv4)
        for step in range(1, n_head):
            part_copy(step).wait_send()
        for out in outs:
            out.wait()

    return kernel


def solution(mesh):
    n_ctx, n_head = mesh.shape["ctx"], mesh.shape["head"]
    n_z = min(8, n_ctx)
    n_y = n_ctx // n_z

    def per_device(queries, keys, values, out_grad, gain, decay_rate, doc_lengths):
        rows, width = queries.shape
        heads = decay_rate.shape[0]
        hd = width // heads
        rows_own = heads * hd // n_ctx
        kernel = make_kernel(n_ctx, n_head, n_y, n_z, rows, heads, hd, width * n_head)
        wide16 = pltpu.VMEM((rows, width), BF16)
        wide32 = pltpu.VMEM((rows, width), F32)
        column = pltpu.VMEM((rows, hd), F32)
        slices = pltpu.VMEM((n_ctx, rows_own, hd), F32)
        dma = pltpu.SemaphoreType.DMA
        out = jax.ShapeDtypeStruct((rows, width), BF16)
        anywhere = pl.BlockSpec(memory_space=pl.ANY)
        scalars = pl.BlockSpec(memory_space=pltpu.SMEM)
        return pl.pallas_call(
            kernel,
            out_shape=(out,) * 4,
            in_specs=[scalars, scalars, pl.BlockSpec(memory_space=pltpu.VMEM)] + [anywhere] * 4,
            out_specs=(anywhere,) * 4,
            scratch_shapes=[wide16] * 8
            + [slices] * 8
            + [
                pltpu.VMEM((heads, rows, rows), BF16),
                wide32,
                wide16,
                pltpu.VMEM((rows, rows), F32),
                column,
                column,
                column,
                column,
                pltpu.VMEM((8, rows), F32),
                pltpu.VMEM((n_head, 8, rows), F32),
                wide32,
                wide32,
                pltpu.VMEM((n_ctx, hd), F32),
                dma((4,)),
                dma((4,)),
            ]
            + [dma((n_ctx,))] * 8
            + [dma((n_head,))] * 2,
            compiler_params=pltpu.CompilerParams(
                collective_id=0, has_side_effects=True, vmem_limit_bytes=56 * 2**20
            ),
        )(doc_lengths, decay_rate, gain.reshape(heads, hd), queries, keys, values, out_grad)

    in_specs = (P("ctx", "head"),) * 4 + (P("head"), P("head"), P())
    return jax.shard_map(
        per_device, mesh=mesh, in_specs=in_specs, out_specs=(P("ctx", "head"),) * 4, check_vma=False
    )
```

```python
import jax
import jax.numpy as jnp
from jax import lax
from jax.experimental import pallas as pl
from jax.experimental.pallas import tpu as pltpu
from jax.sharding import PartitionSpec as P

EPSILON = 1e-05
FAR = 1e30
TILE = 256
UNROLL = 2
MESH = pl.DeviceIdType.MESH
F32, BF16 = jnp.float32, jnp.bfloat16


def matmul(a, b):
    return lax.dot_general(a, b, (((1,), (0,)), ((), ())), preferred_element_type=F32)


def matmul_t(a, b):
    return lax.dot_general(a, b, (((1,), (1,)), ((), ())), preferred_element_type=F32)


def halves(x):
    high = x.astype(BF16)
    low = (x - high.astype(F32)).astype(BF16)
    return high, low


def twice(x):
    return jnp.concatenate([x, x], axis=1)


def make_kernel(n_ctx, n_head, n_y, n_z, rows, heads, hd, features):
    rows_own = heads * hd // n_ctx
    owners = hd // rows_own
    away = [(dy, dz) for dy in range(n_y) for dz in range(n_z) if (dy, dz) != (0, 0)]
    away.sort(key=lambda d: -(min(d[0], n_y - d[0]) + 1.01 * min(d[1], n_z - d[1])))

    def kernel(
        lengths, rates, gain, q_hbm, k_hbm, v_hbm, g_hbm,
        normed, qg, kg, vg,
        q, k, v, g,
        local1, inbox1, outbox1, state1, local2, inbox2, outbox2, state2,
        weights, attended, grad_out, spacing, entry_far, exit_far,
        square_acc, dot_acc, part, parts, key_part, value_part, carry_table,
        in_sem, send1, recv1, send2, recv2, send3, recv3, send4, recv4, send_p, recv_p,
    ):
        me = lax.axis_index("ctx")
        me_h = lax.axis_index("head")
        y, z = me // n_z, me % n_z
        peers = [((y + dy) % n_y) * n_z + (z + dz) % n_z for dy, dz in away]

        loads = [
            pltpu.make_async_copy(src, dst, in_sem.at[i])
            for i, (src, dst) in enumerate(((k_hbm, k), (v_hbm, v), (q_hbm, q), (g_hbm, g)))
        ]
        for load in loads:
            load.start()
        barrier = pltpu.get_barrier_semaphore()
        for peer in peers:
            pl.semaphore_signal(barrier, inc=1, device_id={"ctx": peer}, device_id_type=MESH)
        for step in range(1, n_head):
            pl.semaphore_signal(
                barrier, inc=1, device_id={"head": (me_h + step) % n_head}, device_id_type=MESH
            )

        ends = []
        total = jnp.int32(0)
        for j in range(lengths.shape[0]):
            total = total + lengths[j]
            ends.append(total)

        def doc_of(position):
            count = (position >= ends[0]).astype(jnp.int32)
            for end in ends[1:]:
                count = count + (position >= end).astype(jnp.int32)
            return count

        start = me * rows
        last_doc = doc_of(start + rows - 1)
        before_doc = jnp.where(start > 0, doc_of(start - 1), -1)
        offset = lax.broadcasted_iota(jnp.int32, (rows, hd), 0)
        doc_col = doc_of(start + offset)
        offset_f = offset.astype(F32)
        entry_far[...] = jnp.where(doc_col == before_doc, offset_f + 1.0, FAR)
        exit_far[...] = jnp.where(doc_col == last_doc, rows - 1.0 - offset_f, FAR)

        def decay_row(h):
            rate = rates[h].astype(F32)
            return -jnp.exp2(jnp.full((1, hd), 1.0, F32) * (rate * -0.5))

        def cols(h):
            return pl.ds(pl.multiple_of(h * hd, hd), hd)

        own_head = me // owners

        def far_first(i):
            return (own_head + heads // 2 + i) % heads

        block = lax.broadcasted_iota(jnp.int32, (n_ctx, hd), 0)
        inside = jnp.zeros((n_ctx, hd), jnp.int32)
        for end in ends:
            hit = (end >= block * rows) & (end < block * rows + rows)
            inside = inside + hit.astype(jnp.int32)
        whole = (inside == 0) & (block > 0)
        carry_table[...] = jnp.where(whole, jnp.exp(decay_row(own_head) * float(rows)), 0.0)

        loads[0].wait()
        loads[1].wait()

        @pl.loop(0, heads)
        def _(h):
            fade = jnp.exp(exit_far[...] * decay_row(h))
            scaled = (k[:, cols(h)].astype(F32) * fade).astype(BF16)
            state = matmul(scaled.T, v[:, cols(h)])
            local1[pl.ds(h * owners, owners)] = state.reshape(owners, rows_own, hd)

        pl.semaphore_wait(barrier, n_ctx - 1 + n_head - 1)

        def spread(src, dst, send, recv):
            for peer in peers:
                pltpu.make_async_remote_copy(
                    src_ref=src.at[peer], dst_ref=dst.at[me], send_sem=send.at[peer],
                    recv_sem=recv.at[me], device_id={"ctx": peer}, device_id_type=MESH,
                ).start()

        def spread_head(h, src, dst, send, recv):
            for piece in range(owners):
                peer = h * owners + piece

                @pl.when(peer != me)
                def _():
                    pltpu.make_async_remote_copy(
                        src_ref=src.at[peer], dst_ref=dst.at[me], send_sem=send.at[peer],
                        recv_sem=recv.at[me], device_id={"ctx": peer}, device_id_type=MESH,
                    ).start()

        def arrived_head(h, dst, recv, send):
            for piece in range(owners):
                peer = h * owners + piece

                @pl.when(peer != me)
                def _():
                    arrived(dst, recv, send, peer)

        def arrived(dst, recv, send, slot):
            pltpu.make_async_remote_copy(
                src_ref=dst.at[slot], dst_ref=dst.at[slot], send_sem=send.at[slot],
                recv_sem=recv.at[slot], device_id={"ctx": slot}, device_id_type=MESH,
            ).wait_recv()

        def arrived_all(dst, recv, send):
            for peer in peers:
                arrived(dst, recv, send, peer)

        def left_all(src, dst, send, recv):
            for peer in peers:
                pltpu.make_async_remote_copy(
                    src_ref=src.at[peer], dst_ref=dst.at[me], send_sem=send.at[peer],
                    recv_sem=recv.at[me], device_id={"ctx": peer}, device_id_type=MESH,
                ).wait_send()

        spread(local1, inbox1, send1, recv1)
        inbox1[pl.ds(me, 1)] = local1[pl.ds(me, 1)]

        row_pos = start + lax.broadcasted_iota(jnp.int32, (8, rows), 1)
        doc_row = doc_of(row_pos)[0:1]
        for c in range(rows // hd):
            piece = slice(c * hd, (c + 1) * hd)
            gap = offset - (lax.broadcasted_iota(jnp.int32, (rows, hd), 1) + c * hd)
            same = (doc_col == doc_row[:, piece]) & (gap >= 0)
            spacing[:, piece] = jnp.where(same, gap.astype(F32), FAR)
        loads[2].wait()
        loads[3].wait()

        tiles = [(i * TILE, (i + 1) * TILE) for i in range(rows // TILE)]

        def wide(row, n):
            return jnp.concatenate([row] * (n // hd), axis=1)

        def forward(h):
            rate = decay_row(h)
            key_h, value_h = k[:, cols(h)], v[:, cols(h)]
            for lo, hi in tiles:
                scores = matmul_t(q[lo:hi, cols(h)], key_h[:hi])
                inner = jnp.exp(spacing[lo:hi, :hi] * wide(rate, hi))
                w = (scores * inner).astype(BF16)
                weights[h, lo:hi, :hi] = w
                attended[lo:hi, cols(h)] = matmul(w, value_h[:hi])

        half = heads // 2

        @pl.loop(0, half)
        def _(h):
            forward(h)

        arrived_all(inbox1, recv1, send1)

        def prefix(inbox, outbox, state, reverse):
            def lap(i, carried):
                j = n_ctx - 1 - i if reverse else i
                outbox[pl.ds(j, 1)] = carried[None]
                return carried * carry_table[pl.ds(j, 1), :] + inbox[j]

            lax.fori_loop(0, n_ctx, lap, jnp.zeros((rows_own, hd), F32))
            state[pl.ds(me, 1)] = outbox[pl.ds(me, 1)]

        prefix(inbox1, outbox1, state1, False)
        spread(outbox1, state1, send2, recv2)

        @pl.loop(half, heads)
        def _(h):
            forward(h)

        square_acc[...] = jnp.zeros_like(square_acc)
        dot_acc[...] = jnp.zeros_like(dot_acc)

        @pl.loop(0, heads, unroll=UNROLL)
        def _(i):
            h = far_first(i)
            arrived_head(h, state1, recv2, send2)
            high, low = halves(state1[pl.ds(h * owners, owners)].reshape(hd, hd))
            far = matmul(twice(q[:, cols(h)]), jnp.concatenate([high, low], axis=0))
            fade = jnp.exp(entry_far[...] * decay_row(h))
            att = attended[:, cols(h)] + fade * far
            attended[:, cols(h)] = att
            square_acc[...] += att * att
            dot_acc[...] += (g[:, cols(h)].astype(F32) * gain[pl.ds(h, 1), :]) * att

        def row_sums(x):
            return jnp.broadcast_to(jnp.sum(x, axis=1, keepdims=True), x.shape).T[0:8]

        first = lax.broadcasted_iota(jnp.int32, (8, rows), 0) < 4
        part[...] = jnp.where(first, row_sums(square_acc[...]), row_sums(dot_acc[...]))

        def part_copy(step):
            peer = (me_h + step) % n_head
            return pltpu.make_async_remote_copy(
                src_ref=part, dst_ref=parts.at[me_h], send_sem=send_p.at[peer],
                recv_sem=recv_p.at[me_h], device_id={"head": peer}, device_id_type=MESH,
            )

        for step in range(1, n_head):
            part_copy(step).start()
        parts[pl.ds(me_h, 1)] = part[...][None]
        for step in range(1, n_head):
            peer = (me_h + step) % n_head
            pltpu.make_async_remote_copy(
                src_ref=part, dst_ref=parts.at[peer], send_sem=send_p.at[peer],
                recv_sem=recv_p.at[peer], device_id={"head": peer}, device_id_type=MESH,
            ).wait_recv()
        total_part = parts[0]
        for slot in range(1, n_head):
            total_part = total_part + parts[slot]
        inv_row = lax.rsqrt(total_part[0:4] / features + EPSILON)
        pull_row = (inv_row * inv_row) * total_part[4:8] / features
        both = jnp.concatenate([inv_row, pull_row], axis=0)
        turned = jnp.concatenate([both] * (hd // 8), axis=0).T
        inv = jnp.broadcast_to(turned[:, 0:1], (rows, hd))
        pull = jnp.broadcast_to(turned[:, 4:5], (rows, hd))
        square_acc[...] = inv
        dot_acc[...] = pull

        def local_grad(i):
            h = far_first(i)
            inv, pull = square_acc[...], dot_acc[...]
            att = attended[:, cols(h)]
            gain_h = gain[pl.ds(h, 1), :]
            grad_gain = g[:, cols(h)].astype(F32) * gain_h
            normed[:, cols(h)] = (att * inv * gain_h).astype(BF16)
            grad_h = (inv * (grad_gain - att * pull)).astype(BF16)
            grad_out[:, cols(h)] = grad_h
            fade = jnp.exp(entry_far[...] * decay_row(h))
            scaled = (q[:, cols(h)].astype(F32) * fade).astype(BF16)
            local2[pl.ds(h * owners, owners)] = matmul(scaled.T, grad_h).reshape(
                owners, rows_own, hd
            )

        local_grad(0)

        @pl.loop(1, heads, unroll=True)
        def _(i):
            local_grad(i)
            spread_head(far_first(i - 1), local2, inbox2, send3, recv3)

        spread_head(far_first(heads - 1), local2, inbox2, send3, recv3)
        inbox2[pl.ds(me, 1)] = local2[pl.ds(me, 1)]

        def backward(h):
            rate = decay_row(h)
            grad_h, key_h, value_h = grad_out[:, cols(h)], k[:, cols(h)], v[:, cols(h)]
            query_t, grad_t = q[:, cols(h)].T, grad_h.T
            high, low = halves(state1[pl.ds(h * owners, owners)].reshape(hd, hd))
            far = matmul_t(twice(grad_h), jnp.concatenate([high, low], axis=1))
            fade = jnp.exp(entry_far[...] * rate)
            far = far * fade
            key_sum = jnp.zeros((hd, rows), F32)
            value_sum = jnp.zeros((hd, rows), F32)
            for lo, hi in tiles:
                scores = matmul_t(grad_h[lo:hi], value_h[:hi])
                inner = jnp.exp(spacing[lo:hi, :hi] * wide(rate, hi))
                gw = (scores * inner).astype(BF16)
                qg[lo:hi, cols(h)] = (matmul(gw, key_h[:hi]) + far[lo:hi]).astype(BF16)
                key_add = matmul(query_t[:, lo:hi], gw)
                value_add = matmul(grad_t[:, lo:hi], weights[h, lo:hi, :hi])
                if hi < rows:
                    rest = jnp.zeros((hd, rows - hi), F32)
                    key_add = jnp.concatenate([key_add, rest], axis=1)
                    value_add = jnp.concatenate([value_add, rest], axis=1)
                key_sum = key_sum + key_add
                value_sum = value_sum + value_add
            key_part[:, cols(h)] = key_sum.T
            value_part[:, cols(h)] = value_sum.T

        @pl.loop(0, half)
        def _(h):
            backward(h)

        arrived_all(inbox2, recv3, send3)
        prefix(inbox2, outbox2, state2, True)
        spread(outbox2, state2, send4, recv4)

        @pl.loop(half, heads)
        def _(h):
            backward(h)


        @pl.loop(0, heads, unroll=UNROLL)
        def _(i):
            h = far_first(i)
            arrived_head(h, state2, recv4, send4)
            high, low = halves(state2[pl.ds(h * owners, owners)].reshape(hd, hd))
            fade = jnp.exp(exit_far[...] * decay_row(h))
            key_far = matmul_t(twice(v[:, cols(h)]), jnp.concatenate([high, low], axis=1))
            value_far = matmul(twice(k[:, cols(h)]), jnp.concatenate([high, low], axis=0))
            kg[:, cols(h)] = (key_part[:, cols(h)] + fade * key_far).astype(BF16)
            vg[:, cols(h)] = (value_part[:, cols(h)] + fade * value_far).astype(BF16)

        left_all(local1, inbox1, send1, recv1)
        left_all(outbox1, state1, send2, recv2)
        left_all(local2, inbox2, send3, recv3)
        left_all(outbox2, state2, send4, recv4)
        for step in range(1, n_head):
            part_copy(step).wait_send()

    return kernel


def solution(mesh):
    n_ctx, n_head = mesh.shape["ctx"], mesh.shape["head"]
    n_z = min(8, n_ctx)
    n_y = n_ctx // n_z

    def per_device(queries, keys, values, out_grad, gain, decay_rate, doc_lengths):
        rows, width = queries.shape
        heads = decay_rate.shape[0]
        hd = width // heads
        rows_own = heads * hd // n_ctx
        kernel = make_kernel(n_ctx, n_head, n_y, n_z, rows, heads, hd, width * n_head)
        wide16 = pltpu.VMEM((rows, width), BF16)
        wide32 = pltpu.VMEM((rows, width), F32)
        column = pltpu.VMEM((rows, hd), F32)
        slices = pltpu.VMEM((n_ctx, rows_own, hd), F32)
        dma = pltpu.SemaphoreType.DMA
        anywhere = pl.BlockSpec(memory_space=pl.ANY)
        scalars = pl.BlockSpec(memory_space=pltpu.SMEM)
        return pl.pallas_call(
            kernel,
            out_shape=(wide16,) * 4,
            in_specs=[scalars, scalars, pl.BlockSpec(memory_space=pltpu.VMEM)] + [anywhere] * 4,
            out_specs=(pl.BlockSpec(memory_space=pltpu.VMEM),) * 4,
            scratch_shapes=[wide16] * 4
            + [slices] * 8
            + [
                pltpu.VMEM((heads, rows, rows), BF16),
                wide32,
                wide16,
                pltpu.VMEM((rows, rows), F32),
                column,
                column,
                column,
                column,
                pltpu.VMEM((8, rows), F32),
                pltpu.VMEM((n_head, 8, rows), F32),
                wide32,
                wide32,
                pltpu.VMEM((n_ctx, hd), F32),
                dma((4,)),
            ]
            + [dma((n_ctx,))] * 8
            + [dma((n_head,))] * 2,
            compiler_params=pltpu.CompilerParams(
                collective_id=0, has_side_effects=True, vmem_limit_bytes=56 * 2**20
            ),
        )(doc_lengths, decay_rate, gain.reshape(heads, hd), queries, keys, values, out_grad)

    in_specs = (P("ctx", "head"),) * 4 + (P("head"), P("head"), P())
    return jax.shard_map(
        per_device, mesh=mesh, in_specs=in_specs, out_specs=(P("ctx", "head"),) * 4, check_vma=False
    )
```

```python
import jax
import jax.numpy as jnp
from jax import lax
from jax.experimental import pallas as pl
from jax.experimental.pallas import tpu as pltpu
from jax.sharding import PartitionSpec as P

EPSILON = 1e-05
FAR = 1e30
TILE = 256
UNROLL = 4
MESH = pl.DeviceIdType.MESH
F32, BF16 = jnp.float32, jnp.bfloat16


def matmul(a, b):
    return lax.dot_general(a, b, (((1,), (0,)), ((), ())), preferred_element_type=F32)


def matmul_t(a, b):
    return lax.dot_general(a, b, (((1,), (1,)), ((), ())), preferred_element_type=F32)


def halves(x):
    high = x.astype(BF16)
    low = (x - high.astype(F32)).astype(BF16)
    return high, low


def twice(x):
    return jnp.concatenate([x, x], axis=1)


def make_kernel(n_ctx, n_head, n_y, n_z, rows, heads, hd, features):
    rows_own = heads * hd // n_ctx
    owners = hd // rows_own
    away = [(dy, dz) for dy in range(n_y) for dz in range(n_z) if (dy, dz) != (0, 0)]
    away.sort(key=lambda d: -(min(d[0], n_y - d[0]) + 1.01 * min(d[1], n_z - d[1])))

    def kernel(
        lengths, rates, gain, q_hbm, k_hbm, v_hbm, g_hbm,
        normed, qg, kg, vg,
        q, k, v, g,
        local1, inbox1, outbox1, state1, local2, inbox2, outbox2, state2,
        weights, attended, grad_out, spacing, entry_far, exit_far,
        square_acc, dot_acc, part, parts, key_part, value_part, carry_table, query_scaled,
        in_sem, send1, recv1, send2, recv2, send3, recv3, send4, recv4, send_p, recv_p,
    ):
        me = lax.axis_index("ctx")
        me_h = lax.axis_index("head")
        y, z = me // n_z, me % n_z
        peers = [((y + dy) % n_y) * n_z + (z + dz) % n_z for dy, dz in away]

        loads = [
            pltpu.make_async_copy(src, dst, in_sem.at[i])
            for i, (src, dst) in enumerate(((k_hbm, k), (v_hbm, v), (q_hbm, q), (g_hbm, g)))
        ]
        for load in loads:
            load.start()
        barrier = pltpu.get_barrier_semaphore()
        for peer in peers:
            pl.semaphore_signal(barrier, inc=1, device_id={"ctx": peer}, device_id_type=MESH)
        for step in range(1, n_head):
            pl.semaphore_signal(
                barrier, inc=1, device_id={"head": (me_h + step) % n_head}, device_id_type=MESH
            )

        ends = []
        total = jnp.int32(0)
        for j in range(lengths.shape[0]):
            total = total + lengths[j]
            ends.append(total)

        def doc_of(position):
            count = (position >= ends[0]).astype(jnp.int32)
            for end in ends[1:]:
                count = count + (position >= end).astype(jnp.int32)
            return count

        start = me * rows
        last_doc = doc_of(start + rows - 1)
        before_doc = jnp.where(start > 0, doc_of(start - 1), -1)
        offset = lax.broadcasted_iota(jnp.int32, (rows, hd), 0)
        doc_col = doc_of(start + offset)
        offset_f = offset.astype(F32)
        entry_far[...] = jnp.where(doc_col == before_doc, offset_f + 1.0, FAR)
        exit_far[...] = jnp.where(doc_col == last_doc, rows - 1.0 - offset_f, FAR)

        def decay_row(h):
            rate = rates[h].astype(F32)
            return -jnp.exp2(jnp.full((1, hd), 1.0, F32) * (rate * -0.5))

        def cols(h):
            return pl.ds(pl.multiple_of(h * hd, hd), hd)

        own_head = me // owners

        def far_first(i):
            return (own_head + heads // 2 + i) % heads

        block = lax.broadcasted_iota(jnp.int32, (n_ctx, hd), 0)
        inside = jnp.zeros((n_ctx, hd), jnp.int32)
        for end in ends:
            hit = (end >= block * rows) & (end < block * rows + rows)
            inside = inside + hit.astype(jnp.int32)
        whole = (inside == 0) & (block > 0)
        carry_table[...] = jnp.where(whole, jnp.exp(decay_row(own_head) * float(rows)), 0.0)

        loads[0].wait()
        loads[1].wait()

        @pl.loop(0, heads)
        def _(h):
            fade = jnp.exp(exit_far[...] * decay_row(h))
            scaled = (k[:, cols(h)].astype(F32) * fade).astype(BF16)
            state = matmul(scaled.T, v[:, cols(h)])
            local1[pl.ds(h * owners, owners)] = state.reshape(owners, rows_own, hd)

        pl.semaphore_wait(barrier, n_ctx - 1 + n_head - 1)

        def spread(src, dst, send, recv):
            for peer in peers:
                pltpu.make_async_remote_copy(
                    src_ref=src.at[peer], dst_ref=dst.at[me], send_sem=send.at[peer],
                    recv_sem=recv.at[me], device_id={"ctx": peer}, device_id_type=MESH,
                ).start()

        def spread_head(h, src, dst, send, recv):
            for piece in range(owners):
                peer = h * owners + piece

                @pl.when(peer != me)
                def _():
                    pltpu.make_async_remote_copy(
                        src_ref=src.at[peer], dst_ref=dst.at[me], send_sem=send.at[peer],
                        recv_sem=recv.at[me], device_id={"ctx": peer}, device_id_type=MESH,
                    ).start()

        def arrived_head(h, dst, recv, send):
            for piece in range(owners):
                peer = h * owners + piece

                @pl.when(peer != me)
                def _():
                    arrived(dst, recv, send, peer)

        def arrived(dst, recv, send, slot):
            pltpu.make_async_remote_copy(
                src_ref=dst.at[slot], dst_ref=dst.at[slot], send_sem=send.at[slot],
                recv_sem=recv.at[slot], device_id={"ctx": slot}, device_id_type=MESH,
            ).wait_recv()

        def arrived_all(dst, recv, send):
            for peer in peers:
                arrived(dst, recv, send, peer)

        def left_all(src, dst, send, recv):
            for peer in peers:
                pltpu.make_async_remote_copy(
                    src_ref=src.at[peer], dst_ref=dst.at[me], send_sem=send.at[peer],
                    recv_sem=recv.at[me], device_id={"ctx": peer}, device_id_type=MESH,
                ).wait_send()

        spread(local1, inbox1, send1, recv1)
        inbox1[pl.ds(me, 1)] = local1[pl.ds(me, 1)]

        row_pos = start + lax.broadcasted_iota(jnp.int32, (8, rows), 1)
        doc_row = doc_of(row_pos)[0:1]
        for c in range(rows // hd):
            piece = slice(c * hd, (c + 1) * hd)
            gap = offset - (lax.broadcasted_iota(jnp.int32, (rows, hd), 1) + c * hd)
            same = (doc_col == doc_row[:, piece]) & (gap >= 0)
            spacing[:, piece] = jnp.where(same, gap.astype(F32), FAR)
        loads[2].wait()
        loads[3].wait()

        tiles = [(i * TILE, (i + 1) * TILE) for i in range(rows // TILE)]

        def wide(row, n):
            return jnp.concatenate([row] * (n // hd), axis=1)

        def forward(h):
            rate = decay_row(h)
            key_h, value_h = k[:, cols(h)], v[:, cols(h)]
            fade = jnp.exp(entry_far[...] * rate)
            query_scaled[h] = (q[:, cols(h)].astype(F32) * fade).astype(BF16).T
            for lo, hi in tiles:
                scores = matmul_t(q[lo:hi, cols(h)], key_h[:hi])
                inner = jnp.exp(spacing[lo:hi, :hi] * wide(rate, hi))
                w = (scores * inner).astype(BF16)
                weights[h, lo:hi, :hi] = w
                attended[lo:hi, cols(h)] = matmul(w, value_h[:hi])

        half = heads // 2

        @pl.loop(0, half)
        def _(h):
            forward(h)

        arrived_all(inbox1, recv1, send1)

        def prefix(inbox, outbox, state, reverse):
            def lap(i, carried):
                j = n_ctx - 1 - i if reverse else i
                outbox[pl.ds(j, 1)] = carried[None]
                return carried * carry_table[pl.ds(j, 1), :] + inbox[j]

            lax.fori_loop(0, n_ctx, lap, jnp.zeros((rows_own, hd), F32), unroll=4)
            state[pl.ds(me, 1)] = outbox[pl.ds(me, 1)]

        prefix(inbox1, outbox1, state1, False)
        spread(outbox1, state1, send2, recv2)

        @pl.loop(half, heads)
        def _(h):
            forward(h)

        square_acc[...] = jnp.zeros_like(square_acc)
        dot_acc[...] = jnp.zeros_like(dot_acc)

        @pl.loop(0, heads, unroll=UNROLL)
        def _(i):
            h = far_first(i)
            arrived_head(h, state1, recv2, send2)
            high, low = halves(state1[pl.ds(h * owners, owners)].reshape(hd, hd))
            far = matmul(twice(q[:, cols(h)]), jnp.concatenate([high, low], axis=0))
            fade = jnp.exp(entry_far[...] * decay_row(h))
            att = attended[:, cols(h)] + fade * far
            attended[:, cols(h)] = att
            square_acc[...] += att * att
            dot_acc[...] += (g[:, cols(h)].astype(F32) * gain[pl.ds(h, 1), :]) * att

        def row_sums(x):
            return jnp.broadcast_to(jnp.sum(x, axis=1, keepdims=True), x.shape).T[0:8]

        first = lax.broadcasted_iota(jnp.int32, (8, rows), 0) < 4
        part[...] = jnp.where(first, row_sums(square_acc[...]), row_sums(dot_acc[...]))

        def part_copy(step):
            peer = (me_h + step) % n_head
            return pltpu.make_async_remote_copy(
                src_ref=part, dst_ref=parts.at[me_h], send_sem=send_p.at[peer],
                recv_sem=recv_p.at[me_h], device_id={"head": peer}, device_id_type=MESH,
            )

        for step in range(1, n_head):
            part_copy(step).start()
        parts[pl.ds(me_h, 1)] = part[...][None]
        for step in range(1, n_head):
            peer = (me_h + step) % n_head
            pltpu.make_async_remote_copy(
                src_ref=part, dst_ref=parts.at[peer], send_sem=send_p.at[peer],
                recv_sem=recv_p.at[peer], device_id={"head": peer}, device_id_type=MESH,
            ).wait_recv()
        total_part = parts[0]
        for slot in range(1, n_head):
            total_part = total_part + parts[slot]
        inv_row = lax.rsqrt(total_part[0:4] / features + EPSILON)
        pull_row = (inv_row * inv_row) * total_part[4:8] / features
        both = jnp.concatenate([inv_row, pull_row], axis=0)
        turned = jnp.concatenate([both] * (hd // 8), axis=0).T
        inv = jnp.broadcast_to(turned[:, 0:1], (rows, hd))
        pull = jnp.broadcast_to(turned[:, 4:5], (rows, hd))
        square_acc[...] = inv
        dot_acc[...] = pull

        def local_grad(i):
            h = far_first(i)
            inv, pull = square_acc[...], dot_acc[...]
            att = attended[:, cols(h)]
            gain_h = gain[pl.ds(h, 1), :]
            grad_gain = g[:, cols(h)].astype(F32) * gain_h
            grad_h = (inv * (grad_gain - att * pull)).astype(BF16)
            grad_out[:, cols(h)] = grad_h
            local2[pl.ds(h * owners, owners)] = matmul(query_scaled[h], grad_h).reshape(
                owners, rows_own, hd
            )

        local_grad(0)

        @pl.loop(1, heads, unroll=True)
        def _(i):
            local_grad(i)
            spread_head(far_first(i - 1), local2, inbox2, send3, recv3)

        spread_head(far_first(heads - 1), local2, inbox2, send3, recv3)
        inbox2[pl.ds(me, 1)] = local2[pl.ds(me, 1)]

        def backward(h):
            rate = decay_row(h)
            gain_h = gain[pl.ds(h, 1), :]
            normed[:, cols(h)] = (attended[:, cols(h)] * square_acc[...] * gain_h).astype(BF16)
            grad_h, key_h, value_h = grad_out[:, cols(h)], k[:, cols(h)], v[:, cols(h)]
            query_t, grad_t = q[:, cols(h)].T, grad_h.T
            high, low = halves(state1[pl.ds(h * owners, owners)].reshape(hd, hd))
            far = matmul_t(twice(grad_h), jnp.concatenate([high, low], axis=1))
            fade = jnp.exp(entry_far[...] * rate)
            far = far * fade
            key_sum = jnp.zeros((hd, rows), F32)
            value_sum = jnp.zeros((hd, rows), F32)
            for lo, hi in tiles:
                scores = matmul_t(grad_h[lo:hi], value_h[:hi])
                inner = jnp.exp(spacing[lo:hi, :hi] * wide(rate, hi))
                gw = (scores * inner).astype(BF16)
                qg[lo:hi, cols(h)] = (matmul(gw, key_h[:hi]) + far[lo:hi]).astype(BF16)
                key_add = matmul(query_t[:, lo:hi], gw)
                value_add = matmul(grad_t[:, lo:hi], weights[h, lo:hi, :hi])
                if hi < rows:
                    rest = jnp.zeros((hd, rows - hi), F32)
                    key_add = jnp.concatenate([key_add, rest], axis=1)
                    value_add = jnp.concatenate([value_add, rest], axis=1)
                key_sum = key_sum + key_add
                value_sum = value_sum + value_add
            key_part[:, cols(h)] = key_sum.T
            value_part[:, cols(h)] = value_sum.T

        @pl.loop(0, half)
        def _(h):
            backward(h)

        arrived_all(inbox2, recv3, send3)
        prefix(inbox2, outbox2, state2, True)
        spread(outbox2, state2, send4, recv4)

        @pl.loop(half, heads)
        def _(h):
            backward(h)


        @pl.loop(0, heads, unroll=UNROLL)
        def _(i):
            h = far_first(i)
            arrived_head(h, state2, recv4, send4)
            high, low = halves(state2[pl.ds(h * owners, owners)].reshape(hd, hd))
            fade = jnp.exp(exit_far[...] * decay_row(h))
            key_far = matmul_t(twice(v[:, cols(h)]), jnp.concatenate([high, low], axis=1))
            value_far = matmul(twice(k[:, cols(h)]), jnp.concatenate([high, low], axis=0))
            kg[:, cols(h)] = (key_part[:, cols(h)] + fade * key_far).astype(BF16)
            vg[:, cols(h)] = (value_part[:, cols(h)] + fade * value_far).astype(BF16)

        left_all(local1, inbox1, send1, recv1)
        left_all(outbox1, state1, send2, recv2)
        left_all(local2, inbox2, send3, recv3)
        left_all(outbox2, state2, send4, recv4)
        for step in range(1, n_head):
            part_copy(step).wait_send()

    return kernel


def solution(mesh):
    n_ctx, n_head = mesh.shape["ctx"], mesh.shape["head"]
    n_z = min(8, n_ctx)
    n_y = n_ctx // n_z

    def per_device(queries, keys, values, out_grad, gain, decay_rate, doc_lengths):
        rows, width = queries.shape
        heads = decay_rate.shape[0]
        hd = width // heads
        rows_own = heads * hd // n_ctx
        kernel = make_kernel(n_ctx, n_head, n_y, n_z, rows, heads, hd, width * n_head)
        wide16 = pltpu.VMEM((rows, width), BF16)
        wide32 = pltpu.VMEM((rows, width), F32)
        column = pltpu.VMEM((rows, hd), F32)
        slices = pltpu.VMEM((n_ctx, rows_own, hd), F32)
        dma = pltpu.SemaphoreType.DMA
        anywhere = pl.BlockSpec(memory_space=pl.ANY)
        scalars = pl.BlockSpec(memory_space=pltpu.SMEM)
        return pl.pallas_call(
            kernel,
            out_shape=(wide16,) * 4,
            in_specs=[scalars, scalars, pl.BlockSpec(memory_space=pltpu.VMEM)] + [anywhere] * 4,
            out_specs=(pl.BlockSpec(memory_space=pltpu.VMEM),) * 4,
            scratch_shapes=[wide16] * 4
            + [slices] * 8
            + [
                pltpu.VMEM((heads, rows, rows), BF16),
                wide32,
                wide16,
                pltpu.VMEM((rows, rows), F32),
                column,
                column,
                column,
                column,
                pltpu.VMEM((8, rows), F32),
                pltpu.VMEM((n_head, 8, rows), F32),
                wide32,
                wide32,
                pltpu.VMEM((n_ctx, hd), F32),
                pltpu.VMEM((heads, hd, rows), BF16),
                dma((4,)),
            ]
            + [dma((n_ctx,))] * 8
            + [dma((n_head,))] * 2,
            compiler_params=pltpu.CompilerParams(
                collective_id=0, has_side_effects=True, vmem_limit_bytes=56 * 2**20
            ),
        )(doc_lengths, decay_rate, gain.reshape(heads, hd), queries, keys, values, out_grad)

    in_specs = (P("ctx", "head"),) * 4 + (P("head"), P("head"), P())
    return jax.shard_map(
        per_device, mesh=mesh, in_specs=in_specs, out_specs=(P("ctx", "head"),) * 4, check_vma=False
    )
```

```python
import jax
import jax.numpy as jnp
from jax import lax
from jax.experimental import pallas as pl
from jax.experimental.pallas import tpu as pltpu
from jax.sharding import PartitionSpec as P

EPSILON = 1e-05
FAR = 1e30
TILE = 256
UNROLL = 8
MESH = pl.DeviceIdType.MESH
F32, BF16 = jnp.float32, jnp.bfloat16


def matmul(a, b):
    return lax.dot_general(a, b, (((1,), (0,)), ((), ())), preferred_element_type=F32)


def matmul_t(a, b):
    return lax.dot_general(a, b, (((1,), (1,)), ((), ())), preferred_element_type=F32)


def halves(x):
    high = x.astype(BF16)
    low = (x - high.astype(F32)).astype(BF16)
    return high, low


def twice(x):
    return jnp.concatenate([x, x], axis=1)


def make_kernel(n_ctx, n_head, n_y, n_z, rows, heads, hd, features):
    rows_own = heads * hd // n_ctx
    owners = hd // rows_own
    away = [(dy, dz) for dy in range(n_y) for dz in range(n_z) if (dy, dz) != (0, 0)]
    away.sort(key=lambda d: -(min(d[0], n_y - d[0]) + 1.01 * min(d[1], n_z - d[1])))

    def kernel(
        lengths, rates, gain, q_hbm, k_hbm, v_hbm, g_hbm,
        normed, qg, kg, vg,
        q, k, v, g,
        local1, inbox1, outbox1, state1, local2, inbox2, outbox2, state2,
        weights, attended, grad_out, spacing, entry_far, exit_far,
        square_acc, dot_acc, part, parts, key_part, value_part, carry_table, query_scaled,
        in_sem, send1, recv1, send2, recv2, send3, recv3, send4, recv4, send_p, recv_p,
    ):
        me = lax.axis_index("ctx")
        me_h = lax.axis_index("head")
        y, z = me // n_z, me % n_z
        peers = [((y + dy) % n_y) * n_z + (z + dz) % n_z for dy, dz in away]

        loads = [
            pltpu.make_async_copy(src, dst, in_sem.at[i])
            for i, (src, dst) in enumerate(((k_hbm, k), (v_hbm, v), (q_hbm, q), (g_hbm, g)))
        ]
        for load in loads:
            load.start()
        barrier = pltpu.get_barrier_semaphore()
        for peer in peers:
            pl.semaphore_signal(barrier, inc=1, device_id={"ctx": peer}, device_id_type=MESH)
        for step in range(1, n_head):
            pl.semaphore_signal(
                barrier, inc=1, device_id={"head": (me_h + step) % n_head}, device_id_type=MESH
            )

        ends = []
        total = jnp.int32(0)
        for j in range(lengths.shape[0]):
            total = total + lengths[j]
            ends.append(total)

        def doc_of(position):
            count = (position >= ends[0]).astype(jnp.int32)
            for end in ends[1:]:
                count = count + (position >= end).astype(jnp.int32)
            return count

        start = me * rows
        last_doc = doc_of(start + rows - 1)
        before_doc = jnp.where(start > 0, doc_of(start - 1), -1)
        offset = lax.broadcasted_iota(jnp.int32, (rows, hd), 0)
        doc_col = doc_of(start + offset)
        offset_f = offset.astype(F32)
        entry_far[...] = jnp.where(doc_col == before_doc, offset_f + 1.0, FAR)
        exit_far[...] = jnp.where(doc_col == last_doc, rows - 1.0 - offset_f, FAR)

        def decay_row(h):
            rate = rates[h].astype(F32)
            return -jnp.exp2(jnp.full((1, hd), 1.0, F32) * (rate * -0.5))

        def cols(h):
            return pl.ds(pl.multiple_of(h * hd, hd), hd)

        own_head = me // owners

        def far_first(i):
            return (own_head + heads // 2 + i) % heads

        block = lax.broadcasted_iota(jnp.int32, (n_ctx, hd), 0)
        inside = jnp.zeros((n_ctx, hd), jnp.int32)
        for end in ends:
            hit = (end >= block * rows) & (end < block * rows + rows)
            inside = inside + hit.astype(jnp.int32)
        whole = (inside == 0) & (block > 0)
        carry_table[...] = jnp.where(whole, jnp.exp(decay_row(own_head) * float(rows)), 0.0)

        loads[0].wait()
        loads[1].wait()

        @pl.loop(0, heads)
        def _(h):
            fade = jnp.exp(exit_far[...] * decay_row(h))
            scaled = (k[:, cols(h)].astype(F32) * fade).astype(BF16)
            state = matmul(scaled.T, v[:, cols(h)])
            local1[pl.ds(h * owners, owners)] = state.reshape(owners, rows_own, hd)

        pl.semaphore_wait(barrier, n_ctx - 1 + n_head - 1)

        def spread(src, dst, send, recv):
            for peer in peers:
                pltpu.make_async_remote_copy(
                    src_ref=src.at[peer], dst_ref=dst.at[me], send_sem=send.at[peer],
                    recv_sem=recv.at[me], device_id={"ctx": peer}, device_id_type=MESH,
                ).start()

        def spread_head(h, src, dst, send, recv):
            for piece in range(owners):
                peer = h * owners + piece

                @pl.when(peer != me)
                def _():
                    pltpu.make_async_remote_copy(
                        src_ref=src.at[peer], dst_ref=dst.at[me], send_sem=send.at[peer],
                        recv_sem=recv.at[me], device_id={"ctx": peer}, device_id_type=MESH,
                    ).start()

        def arrived_head(h, dst, recv, send):
            for piece in range(owners):
                peer = h * owners + piece

                @pl.when(peer != me)
                def _():
                    arrived(dst, recv, send, peer)

        def arrived(dst, recv, send, slot):
            pltpu.make_async_remote_copy(
                src_ref=dst.at[slot], dst_ref=dst.at[slot], send_sem=send.at[slot],
                recv_sem=recv.at[slot], device_id={"ctx": slot}, device_id_type=MESH,
            ).wait_recv()

        def arrived_all(dst, recv, send):
            for peer in peers:
                arrived(dst, recv, send, peer)

        def left_all(src, dst, send, recv):
            for peer in peers:
                pltpu.make_async_remote_copy(
                    src_ref=src.at[peer], dst_ref=dst.at[me], send_sem=send.at[peer],
                    recv_sem=recv.at[me], device_id={"ctx": peer}, device_id_type=MESH,
                ).wait_send()

        spread(local1, inbox1, send1, recv1)
        inbox1[pl.ds(me, 1)] = local1[pl.ds(me, 1)]

        row_pos = start + lax.broadcasted_iota(jnp.int32, (8, rows), 1)
        doc_row = doc_of(row_pos)[0:1]
        for c in range(rows // hd):
            piece = slice(c * hd, (c + 1) * hd)
            gap = offset - (lax.broadcasted_iota(jnp.int32, (rows, hd), 1) + c * hd)
            same = (doc_col == doc_row[:, piece]) & (gap >= 0)
            spacing[:, piece] = jnp.where(same, gap.astype(F32), FAR)
        loads[2].wait()
        loads[3].wait()

        tiles = [(i * TILE, (i + 1) * TILE) for i in range(rows // TILE)]

        def wide(row, n):
            return jnp.concatenate([row] * (n // hd), axis=1)

        def forward(h):
            rate = decay_row(h)
            key_h, value_h = k[:, cols(h)], v[:, cols(h)]
            fade = jnp.exp(entry_far[...] * rate)
            query_scaled[h] = (q[:, cols(h)].astype(F32) * fade).astype(BF16).T
            for lo, hi in tiles:
                scores = matmul_t(q[lo:hi, cols(h)], key_h[:hi])
                inner = jnp.exp(spacing[lo:hi, :hi] * wide(rate, hi))
                w = (scores * inner).astype(BF16)
                weights[h, lo:hi, :hi] = w
                attended[lo:hi, cols(h)] = matmul(w, value_h[:hi])

        half = heads // 2

        @pl.loop(0, half)
        def _(h):
            forward(h)

        arrived_all(inbox1, recv1, send1)

        def prefix(inbox, outbox, state, reverse):
            def lap(i, carried):
                j = n_ctx - 1 - i if reverse else i
                outbox[pl.ds(j, 1)] = carried[None]
                return carried * carry_table[pl.ds(j, 1), :] + inbox[j]

            lax.fori_loop(0, n_ctx, lap, jnp.zeros((rows_own, hd), F32), unroll=4)
            state[pl.ds(me, 1)] = outbox[pl.ds(me, 1)]

        prefix(inbox1, outbox1, state1, False)
        spread(outbox1, state1, send2, recv2)

        @pl.loop(half, heads)
        def _(h):
            forward(h)

        square_acc[...] = jnp.zeros_like(square_acc)
        dot_acc[...] = jnp.zeros_like(dot_acc)

        @pl.loop(0, heads, unroll=UNROLL)
        def _(i):
            h = far_first(i)
            arrived_head(h, state1, recv2, send2)
            high, low = halves(state1[pl.ds(h * owners, owners)].reshape(hd, hd))
            far = matmul(twice(q[:, cols(h)]), jnp.concatenate([high, low], axis=0))
            fade = jnp.exp(entry_far[...] * decay_row(h))
            att = attended[:, cols(h)] + fade * far
            attended[:, cols(h)] = att
            square_acc[...] += att * att
            dot_acc[...] += (g[:, cols(h)].astype(F32) * gain[pl.ds(h, 1), :]) * att

        def row_sums(x):
            return jnp.broadcast_to(jnp.sum(x, axis=1, keepdims=True), x.shape).T[0:8]

        first = lax.broadcasted_iota(jnp.int32, (8, rows), 0) < 4
        part[...] = jnp.where(first, row_sums(square_acc[...]), row_sums(dot_acc[...]))

        def part_copy(step):
            peer = (me_h + step) % n_head
            return pltpu.make_async_remote_copy(
                src_ref=part, dst_ref=parts.at[me_h], send_sem=send_p.at[peer],
                recv_sem=recv_p.at[me_h], device_id={"head": peer}, device_id_type=MESH,
            )

        for step in range(1, n_head):
            part_copy(step).start()
        parts[pl.ds(me_h, 1)] = part[...][None]
        for step in range(1, n_head):
            peer = (me_h + step) % n_head
            pltpu.make_async_remote_copy(
                src_ref=part, dst_ref=parts.at[peer], send_sem=send_p.at[peer],
                recv_sem=recv_p.at[peer], device_id={"head": peer}, device_id_type=MESH,
            ).wait_recv()
        total_part = parts[0]
        for slot in range(1, n_head):
            total_part = total_part + parts[slot]
        inv_row = lax.rsqrt(total_part[0:4] / features + EPSILON)
        pull_row = (inv_row * inv_row) * total_part[4:8] / features
        both = jnp.concatenate([inv_row, pull_row], axis=0)
        turned = jnp.concatenate([both] * (hd // 8), axis=0).T
        inv = jnp.broadcast_to(turned[:, 0:1], (rows, hd))
        pull = jnp.broadcast_to(turned[:, 4:5], (rows, hd))
        square_acc[...] = inv
        dot_acc[...] = pull

        def local_grad(i):
            h = far_first(i)
            inv, pull = square_acc[...], dot_acc[...]
            att = attended[:, cols(h)]
            gain_h = gain[pl.ds(h, 1), :]
            grad_gain = g[:, cols(h)].astype(F32) * gain_h
            grad_h = (inv * (grad_gain - att * pull)).astype(BF16)
            grad_out[:, cols(h)] = grad_h
            local2[pl.ds(h * owners, owners)] = matmul(query_scaled[h], grad_h).reshape(
                owners, rows_own, hd
            )

        local_grad(0)

        @pl.loop(1, heads, unroll=True)
        def _(i):
            local_grad(i)
            spread_head(far_first(i - 1), local2, inbox2, send3, recv3)

        spread_head(far_first(heads - 1), local2, inbox2, send3, recv3)
        inbox2[pl.ds(me, 1)] = local2[pl.ds(me, 1)]

        def backward(h):
            rate = decay_row(h)
            gain_h = gain[pl.ds(h, 1), :]
            normed[:, cols(h)] = (attended[:, cols(h)] * square_acc[...] * gain_h).astype(BF16)
            grad_h, key_h, value_h = grad_out[:, cols(h)], k[:, cols(h)], v[:, cols(h)]
            query_t, grad_t = q[:, cols(h)].T, grad_h.T
            high, low = halves(state1[pl.ds(h * owners, owners)].reshape(hd, hd))
            far = matmul_t(twice(grad_h), jnp.concatenate([high, low], axis=1))
            fade = jnp.exp(entry_far[...] * rate)
            far = far * fade
            key_sum = jnp.zeros((hd, rows), F32)
            value_sum = jnp.zeros((hd, rows), F32)
            for lo, hi in tiles:
                scores = matmul_t(grad_h[lo:hi], value_h[:hi])
                inner = jnp.exp(spacing[lo:hi, :hi] * wide(rate, hi))
                gw = (scores * inner).astype(BF16)
                qg[lo:hi, cols(h)] = (matmul(gw, key_h[:hi]) + far[lo:hi]).astype(BF16)
                key_add = matmul(query_t[:, lo:hi], gw)
                value_add = matmul(grad_t[:, lo:hi], weights[h, lo:hi, :hi])
                if hi < rows:
                    rest = jnp.zeros((hd, rows - hi), F32)
                    key_add = jnp.concatenate([key_add, rest], axis=1)
                    value_add = jnp.concatenate([value_add, rest], axis=1)
                key_sum = key_sum + key_add
                value_sum = value_sum + value_add
            key_part[:, cols(h)] = key_sum.T
            value_part[:, cols(h)] = value_sum.T

        @pl.loop(0, half)
        def _(h):
            backward(h)

        arrived_all(inbox2, recv3, send3)
        prefix(inbox2, outbox2, state2, True)
        spread(outbox2, state2, send4, recv4)

        @pl.loop(half, heads)
        def _(h):
            backward(h)


        @pl.loop(0, heads, unroll=UNROLL)
        def _(i):
            h = far_first(i)
            arrived_head(h, state2, recv4, send4)
            high, low = halves(state2[pl.ds(h * owners, owners)].reshape(hd, hd))
            fade = jnp.exp(exit_far[...] * decay_row(h))
            key_far = matmul_t(twice(v[:, cols(h)]), jnp.concatenate([high, low], axis=1))
            value_far = matmul(twice(k[:, cols(h)]), jnp.concatenate([high, low], axis=0))
            kg[:, cols(h)] = (key_part[:, cols(h)] + fade * key_far).astype(BF16)
            vg[:, cols(h)] = (value_part[:, cols(h)] + fade * value_far).astype(BF16)

        left_all(local1, inbox1, send1, recv1)
        left_all(outbox1, state1, send2, recv2)
        left_all(local2, inbox2, send3, recv3)
        left_all(outbox2, state2, send4, recv4)
        for step in range(1, n_head):
            part_copy(step).wait_send()

    return kernel


def solution(mesh):
    n_ctx, n_head = mesh.shape["ctx"], mesh.shape["head"]
    n_z = min(8, n_ctx)
    n_y = n_ctx // n_z

    def per_device(queries, keys, values, out_grad, gain, decay_rate, doc_lengths):
        rows, width = queries.shape
        heads = decay_rate.shape[0]
        hd = width // heads
        rows_own = heads * hd // n_ctx
        kernel = make_kernel(n_ctx, n_head, n_y, n_z, rows, heads, hd, width * n_head)
        wide16 = pltpu.VMEM((rows, width), BF16)
        wide32 = pltpu.VMEM((rows, width), F32)
        column = pltpu.VMEM((rows, hd), F32)
        slices = pltpu.VMEM((n_ctx, rows_own, hd), F32)
        dma = pltpu.SemaphoreType.DMA
        anywhere = pl.BlockSpec(memory_space=pl.ANY)
        scalars = pl.BlockSpec(memory_space=pltpu.SMEM)
        return pl.pallas_call(
            kernel,
            out_shape=(wide16,) * 4,
            in_specs=[scalars, scalars, pl.BlockSpec(memory_space=pltpu.VMEM)] + [anywhere] * 4,
            out_specs=(pl.BlockSpec(memory_space=pltpu.VMEM),) * 4,
            scratch_shapes=[wide16] * 4
            + [slices] * 8
            + [
                pltpu.VMEM((heads, rows, rows), BF16),
                wide32,
                wide16,
                pltpu.VMEM((rows, rows), F32),
                column,
                column,
                column,
                column,
                pltpu.VMEM((8, rows), F32),
                pltpu.VMEM((n_head, 8, rows), F32),
                wide32,
                wide32,
                pltpu.VMEM((n_ctx, hd), F32),
                pltpu.VMEM((heads, hd, rows), BF16),
                dma((4,)),
            ]
            + [dma((n_ctx,))] * 8
            + [dma((n_head,))] * 2,
            compiler_params=pltpu.CompilerParams(
                collective_id=0, has_side_effects=True, vmem_limit_bytes=56 * 2**20
            ),
        )(doc_lengths, decay_rate, gain.reshape(heads, hd), queries, keys, values, out_grad)

    in_specs = (P("ctx", "head"),) * 4 + (P("head"), P("head"), P())
    return jax.shard_map(
        per_device, mesh=mesh, in_specs=in_specs, out_specs=(P("ctx", "head"),) * 4, check_vma=False
    )
```
